32 devices in a mesh: batch: 4 (over y, x), seq: 4 (over z), tensor: 2 (over core).
Axes of the slice: x: 2, y: 2, z: 4, core: 2. Of those that a mesh axis runs over, the one named last changes fastest.
Arguments:
- tokens: bfloat16 [4, 512, 2560], P('batch', 'seq'), may hold values from -6 to 6
- segment_ids: int32 [4, 512], P('batch'), may hold values from 0 to 3, never falling along the last dimension, each value on 1 to 256 neighbouring positions
- norm1_gain: float32 [2560], replicated, may hold values from 0.1 to 1.9
- x_weight: bfloat16 [2560, 2560], P('batch', 'tensor'), may hold values from -0.125 to 0.125
- y_weight: bfloat16 [2560, 2560], P('batch', 'tensor'), may hold values from -0.125 to 0.125
- conv_weight: float32 [4, 2560], P(None, 'tensor'), may hold values from -3 to 3
- a_gate_weight: bfloat16 [10, 256, 256], P('tensor'), may hold values from -0.375 to 0.375
- a_gate_bias: float32 [2560], P('tensor'), may hold values from -4 to 4
- in_gate_weight: bfloat16 [10, 256, 256], P('tensor'), may hold values from -0.375 to 0.375
- in_gate_bias: float32 [2560], P('tensor'), may hold values from -4 to 4
- decay_param: float32 [2560], P('tensor'), may hold values from -9 to -4
- out_weight: bfloat16 [2560, 2560], P('tensor', 'batch'), may hold values from -0.3125 to 0.3125
- norm2_gain: float32 [2560], replicated, may hold values from 0.1 to 1.9
- gate_weight: bfloat16 [2560, 7680], P('batch', ('seq', 'tensor')), may hold values from -0.125 to 0.125
- up_weight: bfloat16 [2560, 7680], P('batch', ('seq', 'tensor')), may hold values from -0.125 to 0.125
- down_weight: bfloat16 [7680, 2560], P(('seq', 'tensor'), 'batch'), may hold values from -0.09375 to 0.09375
- out_grad: bfloat16 [4, 512, 2560], P('batch', 'seq'), may hold values from -6 to 6
Outputs:
- block_out: bfloat16 [4, 512, 2560], P('batch', 'seq')
- tokens_grad: float32 [4, 512, 2560], P('batch', 'seq')
- norm1_gain_grad: float32 [2560], replicated
- x_weight_grad: float32 [2560, 2560], P('batch', 'tensor')
- y_weight_grad: float32 [2560, 2560], P('batch', 'tensor')
- conv_weight_grad: float32 [4, 2560], P(None, 'tensor')
- a_gate_weight_grad: float32 [10, 256, 256], P('tensor')
- a_gate_bias_grad: float32 [2560], P('tensor')
- in_gate_weight_grad: float32 [10, 256, 256], P('tensor')
- in_gate_bias_grad: float32 [2560], P('tensor')
- decay_param_grad: float32 [2560], P('tensor')
- out_weight_grad: float32 [2560, 2560], P('tensor', 'batch')
- norm2_gain_grad: float32 [2560], replicated
- gate_weight_grad: float32 [2560, 7680], P('batch', ('seq', 'tensor'))
- up_weight_grad: float32 [2560, 7680], P('batch', ('seq', 'tensor'))
- down_weight_grad: float32 [7680, 2560], P(('seq', 'tensor'), 'batch')
The draws below stay inside these ranges and needn't reach their ends.
Inputs may be any that keep to these rules, and one draw needn't show every extreme that they name: `segment_ids`: along each sequence segment ids never fall, so each document is a contiguous run of at most 256 tokens.
All inputs are finite; a program needn't handle non-finite values.
Results may differ from the reference program's by a relative error of at most 0.019.
Values may be sent and summed in bfloat16 or wider, within the bound.
No kernel may reach another device: no remote copies, remote signals or barrier semaphores. Data moves between devices by JAX's collectives and lax.ppermute only.
A program may use at most 256 MiB of HBM per device.

```python
import math
import jax
import jax.numpy as jnp
import numpy as np
from jax import lax

D = 2560
LRU = 2560
HEADS = 10
BLOCK = 256
FF = 7680
CONV = 4
SEQ_LEN = 512
SEQS = 4
DOCS = 4
DOC_MOST = 256


def draw_decay_param(key, part):
    values = jax.random.uniform(key, (LRU,), jnp.float32, -9.0, -4.0)
    return values


def steps_of(key, dims, cuts, smallest, largest):
    def one(position, shards_of):
        steps = jax.random.uniform(jax.random.fold_in(jax.random.fold_in(key, 6), position), (shards_of,), jnp.float32, smallest / len(cuts), largest / len(cuts))
        return jnp.repeat(jnp.exp(steps), dims[position] // shards_of).reshape((-1,) + (1,) * (len(dims) - position - 1))

    level = one(*cuts[0])
    for cut in cuts[1:]:
        level = level * one(*cut)
    return level


def profile(count, total, limit, skew):
    portions = [(1 << 20) // math.isqrt(standing ** skew) + 1 for standing in range(2, count + 1)]
    surplus, holding = total - limit - (count - 1), [1] * (count - 1)
    while surplus > 0:
        candidates = [i for i in range(count - 1) if holding[i] < limit]
        mass, budget = sum([portions[i] for i in candidates]), surplus
        for i in candidates:
            extra = min(limit - holding[i], max(1, budget * portions[i] // mass), surplus)
            holding[i] = holding[i] + extra
            surplus = surplus - extra
    return np.array([limit] + holding)


def ragged_sizes(stream_key, count, total, limit, lean):
    if count == 2:
        one = jax.random.randint(stream_key, (), max(1, total - limit), min(limit, total - 1) + 1)
        return jnp.stack([one, total - one])
    sizes = jnp.asarray(profile(count, total, limit, lean), jnp.int32)
    twos = (count - 1) // 2
    giver, sink = sizes[1:1 + 2 * twos:2], sizes[2:2 + 2 * twos:2]
    slack = jnp.minimum(giver - 1, limit - sink)
    shifted = jax.random.randint(jax.random.fold_in(stream_key, 1), (twos,), 0, 1 << 20) % (slack + 1)
    sizes = sizes.at[1:1 + 2 * twos:2].set(giver - shifted).at[2:2 + 2 * twos:2].set(sink + shifted)
    return sizes[jax.random.permutation(jax.random.fold_in(stream_key, 2), count)]


def scatter_about(stream_key, shape, deviation, bound, pieces=(), dtype=jnp.bfloat16):
    array = deviation * jax.random.normal(stream_key, shape, jnp.float32)
    if pieces:
        array = array * steps_of(stream_key, shape, pieces, -0.22, 0.18)
    return jnp.clip(array, -bound, bound).astype(dtype)


def setup_inputs(seed: int = 0) -> dict:
    arg_keys = jax.random.split(jax.random.key(seed), 18)
    return {
        "tokens": scatter_about(arg_keys[0], (SEQS, SEQ_LEN, D), 1.0, 6.0, ((0, 4), (1, 4))),
        "segment_ids": jax.vmap(lambda own: jnp.searchsorted(jnp.cumsum(ragged_sizes(own, DOCS, SEQ_LEN, DOC_MOST, 0)), jnp.arange(SEQ_LEN), side="right"))(jax.random.split(arg_keys[1], SEQS)).reshape((SEQS, SEQ_LEN)).astype(jnp.int32),
        "norm1_gain": jnp.clip(1.0 + 0.18 * jax.random.normal(arg_keys[2], (D,), jnp.float32), 0.1, 1.9),
        "x_weight": scatter_about(arg_keys[3], (D, LRU), D ** -0.5, 0.125, ((0, 4), (1, 2))),
        "y_weight": scatter_about(arg_keys[4], (D, LRU), D ** -0.5, 0.125, ((0, 4), (1, 2))),
        "conv_weight": scatter_about(arg_keys[5], (CONV, LRU), 0.5, 3.0, ((1, 2),), jnp.float32),
        "a_gate_weight": scatter_about(arg_keys[6], (HEADS, BLOCK, BLOCK), BLOCK ** -0.5, 0.375, ((0, 2),)),
        "a_gate_bias": scatter_about(arg_keys[7], (LRU,), 1.0, 4.0, ((0, 2),), jnp.float32),
        "in_gate_weight": scatter_about(arg_keys[8], (HEADS, BLOCK, BLOCK), BLOCK ** -0.5, 0.375, ((0, 2),)),
        "in_gate_bias": scatter_about(arg_keys[9], (LRU,), 1.0, 4.0, ((0, 2),), jnp.float32),
        "decay_param": draw_decay_param(jax.random.fold_in(arg_keys[17], 71), 0),
        "out_weight": scatter_about(arg_keys[11], (LRU, D), (LRU // 8) ** -0.5, 0.3125, ((0, 2), (1, 4))),
        "norm2_gain": jnp.clip(1.0 + 0.18 * jax.random.normal(arg_keys[12], (D,), jnp.float32), 0.1, 1.9),
        "gate_weight": scatter_about(arg_keys[13], (D, FF), D ** -0.5, 0.125, ((0, 4), (1, 8))),
        "up_weight": scatter_about(arg_keys[14], (D, FF), D ** -0.5, 0.125, ((0, 4), (1, 8))),
        "down_weight": scatter_about(arg_keys[15], (FF, D), (FF // 2) ** -0.5, 0.09375, ((0, 8), (1, 4))),
        "out_grad": scatter_about(arg_keys[16], (SEQS, SEQ_LEN, D), 1.0, 6.0, ((0, 4), (1, 4))),
    }


@jax.custom_vjp
def low(v):
    return lax.optimization_barrier(v.astype(jnp.bfloat16)).astype(jnp.float32)

@jax.custom_vjp
def low_back(v):
    return v

def low_keep(v):
    return (low(v), None)

def low_pass(kept, grad):
    return (grad,)

def back_keep(v):
    return (v, None)

def back_low(kept, grad):
    return (low(grad),)
low.defvjp(low_keep, low_pass)
low_back.defvjp(back_keep, back_low)
epsilon = 1e-06
highest = lax.Precision.HIGHEST

def gelu_tanh(values):
    return jax.nn.gelu(values, approximate=True)

def rms_scale(values, gain):
    return values * lax.rsqrt(lax.optimization_barrier(jnp.mean(values * values, axis=-1, keepdims=True)) + epsilon) * gain

def pair_step(earlier, later):
    return (earlier[0] * later[0], later[0] * earlier[1] + later[1])

def block_forward(segments, inputs, norm1_gain, x_weight, y_weight, conv_weight, a_gate_weight, a_gate_bias, in_gate_weight, in_gate_bias, decay_param, out_weight, norm2_gain, gate_weight, up_weight, down_weight):
    length = inputs.shape[0]
    normed = low(rms_scale(inputs, norm1_gain))
    x_branch = low(low_back(jnp.dot(normed, x_weight, precision=highest)))
    y_branch = low(low_back(jnp.dot(normed, y_weight, precision=highest)))
    y_gated = gelu_tanh(y_branch)
    marks = jnp.concatenate([jnp.full((CONV - 1,), -1, jnp.int32), segments.astype(jnp.int32)])
    padded = jnp.concatenate([jnp.zeros((CONV - 1, x_branch.shape[1]), jnp.float32), x_branch])
    conv_sum = jnp.zeros_like(x_branch)
    for offset in range(CONV):
        same_doc = (marks[CONV - 1 - offset:CONV - 1 - offset + length] == segments).astype(jnp.float32)
        conv_sum = conv_sum + conv_weight[offset] * padded[CONV - 1 - offset:CONV - 1 - offset + length] * same_doc[:, None]
    conv_out = low(conv_sum)
    blocks_in = conv_out.reshape(length, HEADS, BLOCK)
    gate_a = low_back(jnp.einsum('thi,hij->thj', blocks_in, a_gate_weight, precision=highest).reshape(length, LRU) + a_gate_bias)
    gate_i = low_back(jnp.einsum('thi,hij->thj', blocks_in, in_gate_weight, precision=highest).reshape(length, LRU) + in_gate_bias)
    recur_gate = jax.nn.sigmoid(gate_a)
    input_gate = jax.nn.sigmoid(gate_i)
    reset = segments != marks[CONV - 2:CONV - 2 + length]
    keeping = 1.0 - reset.astype(jnp.float32)
    log_decay = -8.0 * recur_gate * jax.nn.softplus(decay_param)
    decay = jnp.exp(log_decay) * keeping[:, None]
    scaling = jnp.where(reset[:, None], 1.0, jnp.sqrt(-jnp.expm1(2.0 * log_decay)))
    driven = scaling * input_gate * conv_out
    _, states = lax.associative_scan(pair_step, (decay, driven))
    mixed = low(low_back(states * y_gated))
    middle = inputs + low_back(jnp.dot(mixed, out_weight, precision=highest))
    normed_two = low(rms_scale(middle, norm2_gain))
    gate_pre = low_back(jnp.dot(normed_two, gate_weight, precision=highest))
    up_pre = low_back(jnp.dot(normed_two, up_weight, precision=highest))
    hidden = low(low_back(gelu_tanh(gate_pre) * up_pre))
    return middle + jnp.dot(hidden, down_weight, precision=highest)

def reference(tokens, segment_ids, norm1_gain, x_weight, y_weight, conv_weight, a_gate_weight, a_gate_bias, in_gate_weight, in_gate_bias, decay_param, out_weight, norm2_gain, gate_weight, up_weight, down_weight, out_grad):
    weights = tuple((w.astype(jnp.float32) for w in (norm1_gain, x_weight, y_weight, conv_weight, a_gate_weight, a_gate_bias, in_gate_weight, in_gate_bias, decay_param, out_weight, norm2_gain, gate_weight, up_weight, down_weight)))

    def per_sequence(totals, item):
        inputs, segments, cotangent = item

        def forward(values, *params):
            return block_forward(segments, values, *params)
        result, pull = jax.vjp(forward, inputs.astype(jnp.float32), *weights)
        grads = pull(cotangent.astype(jnp.float32))
        totals = tuple((total + grad for total, grad in zip(totals, grads[1:])))
        return (totals, (result.astype(jnp.bfloat16), grads[0]))
    start = tuple((jnp.zeros_like(w) for w in weights))
    totals, (outputs, input_grads) = lax.scan(per_sequence, start, (tokens, segment_ids, out_grad))
    return (outputs, input_grads) + totals
```

```python
import jax
import jax.numpy as jnp
from jax import lax
from jax.experimental import pallas as pl
from jax.experimental.pallas import tpu as pltpu
from jax.sharding import PartitionSpec as P
at_batch = 'batch'
at_seq = 'seq'
at_tensor = 'tensor'
epsilon = 1e-06
longest_document = 256

def swap(piece, axis, bits):
    count = lax.axis_size(axis)
    return lax.ppermute(piece, axis, [(i, i ^ bits) for i in range(count)])

def shifted(piece, axis, by):
    count = lax.axis_size(axis)
    pairs = [(i, i + by) for i in range(count) if 0 <= i + by < count]
    return lax.ppermute(piece, axis, pairs)

def spread(piece, axis, steps=None):
    steps = range(1, lax.axis_size(axis)) if steps is None else steps
    return [piece] + [swap(piece, axis, k) for k in steps]

def trade(pieces, axis, steps=None):
    steps = range(1, lax.axis_size(axis)) if steps is None else steps
    return [pieces[0]] + [swap(piece, axis, k) for piece, k in zip(pieces[1:], steps)]

def near_count():
    size, near = (lax.axis_size(at_batch), 1)
    while near * near < size:
        near *= 2
    return near

def near_steps():
    return range(1, near_count())

def far_steps():
    return range(near_count(), lax.axis_size(at_batch), near_count())

def along_line(piece):
    if lax.axis_size(at_seq) != 4:
        return spread(piece, at_seq)
    across = swap(piece, at_seq, 3)
    beside = swap(piece, at_seq, 1)
    hop = lax.ppermute(piece, at_seq, [(0, 2), (3, 1)])
    relayed = lax.ppermute(across, at_seq, [(2, 3), (1, 0)])
    inner = jnp.logical_or(lax.axis_index(at_seq) == 1, lax.axis_index(at_seq) == 2)
    return [piece, beside, jnp.where(inner, hop, relayed), across]

def onto_line(pieces, gate=None, finish=None):
    if lax.axis_size(at_seq) != 4:
        return total(trade(pieces, at_seq))
    inner = jnp.logical_or(lax.axis_index(at_seq) == 1, lax.axis_index(at_seq) == 2)
    relayed = lax.ppermute(pieces[2], at_seq, [(3, 2), (0, 1)])
    beside = swap(pieces[1], at_seq, 1)
    hop = lax.ppermute(pieces[2], at_seq, [(2, 0), (1, 3)])
    if gate is not None:
        relayed = after(relayed, gate)
    passing = jnp.where(inner, pieces[3].astype(jnp.float32) + relayed.astype(jnp.float32), pieces[3].astype(jnp.float32))
    passing = low(passing)
    across = swap(passing, at_seq, 3)
    if finish is not None:
        across = after(across, *finish())
    return pieces[0].astype(jnp.float32) + beside.astype(jnp.float32) + hop.astype(jnp.float32) + across.astype(jnp.float32)

def after(value, *others):
    return lax.optimization_barrier((value,) + others)[0]

def ordered(relative, axis):
    mine = lax.axis_index(axis)
    stacked = jnp.stack(relative)
    return [lax.dynamic_index_in_dim(stacked, jnp.bitwise_xor(mine, j), 0, keepdims=False) for j in range(len(relative))]

def turned(values):
    count = lax.axis_size(at_batch)
    mine = lax.axis_index(at_batch)
    width = values.shape[-1] // count
    return jnp.concatenate([pick(values, jnp.bitwise_xor(mine, k), width, values.ndim - 1) for k in range(count)], axis=-1)

def total(pieces):
    result = pieces[0].astype(jnp.float32)
    for piece in pieces[1:]:
        result = result + piece.astype(jnp.float32)
    return result

def butterfly(value, axes):
    for axis in axes:
        step = 1
        while step < lax.axis_size(axis):
            other = swap(value, axis, step)
            value = value + other
            step *= 2
    return value

def pick(values, which, size, axis):
    return lax.dynamic_slice_in_dim(values, which * size, size, axis)

def gelu_tanh(values):
    return jax.nn.gelu(values, approximate=True)

def matmul(left, right):
    return jnp.dot(left, right, preferred_element_type=jnp.float32)

def outer_sum(left, right):
    return lax.dot_general(left, right, (((0,), (0,)), ((), ())), preferred_element_type=jnp.float32)

def times_transposed(left, right):
    return lax.dot_general(left, right, (((1,), (1,)), ((), ())), preferred_element_type=jnp.float32)

def low(values):
    return values.astype(jnp.bfloat16)

def rms_scale(values, gain):
    return values * lax.rsqrt(jnp.mean(values * values, axis=-1, keepdims=True) + epsilon) * gain

def norm_back(values, gain, upstream):
    scaling = lax.rsqrt(jnp.mean(values * values, axis=-1, keepdims=True) + epsilon)
    unit_rows = values * scaling
    gain_grad = jnp.sum(upstream * unit_rows, axis=0)
    shaped = upstream * gain
    input_grad = scaling * (shaped - unit_rows * jnp.mean(shaped * unit_rows, axis=-1, keepdims=True))
    return (input_grad, gain_grad)

def whole():
    return pl.BlockSpec(memory_space=pltpu.VMEM)

def run_scan(factor_ref, term_ref, product_ref, state_ref, backward):
    rows, width = term_ref.shape

    def step(position, carried):
        product, state = carried
        row = rows - 1 - position if backward else position
        factor = factor_ref[pl.ds(row + 1, 1), :] if backward else factor_ref[pl.ds(row, 1), :]
        product = factor * product
        state = factor * state + term_ref[pl.ds(row, 1), :]
        product_ref[pl.ds(row, 1), :] = product
        state_ref[pl.ds(row, 1), :] = state
        return (product, state)

    start = (jnp.ones((1, width), jnp.float32), jnp.zeros((1, width), jnp.float32))
    return lax.fori_loop(0, rows, step, start, unroll=8)

def root_of(log_decay):
    half_angle = jnp.tanh(log_decay)
    return jnp.sqrt(-2.0 * half_angle / (1.0 - half_angle))

def lru_ahead(branch, edge, masks, conv_weight, a_weight, a_bias, i_weight, i_bias, softened):
    length, width = branch.shape
    heads, block, _ = a_weight.shape
    taps = conv_weight.shape[0]
    pad = edge.shape[0]

    def kernel(branch_ref, edge_ref, masks_ref, taps_ref, aw_ref, ab_ref, iw_ref, ib_ref, soft_ref, conv_ref, recur_ref, input_ref, product_ref, state_ref, end_ref, extended, decay, driven):
        head = pl.program_id(0)
        extended[pl.ds(0, pad), :] = edge_ref[...].astype(jnp.float32)
        extended[pl.ds(pad, length), :] = branch_ref[...].astype(jnp.float32)
        total_conv = jnp.zeros((length, block), jnp.float32)
        for k in range(taps):
            total_conv = total_conv + taps_ref[k:k + 1, :] * extended[pl.ds(pad - k, length), :] * masks_ref[:, k:k + 1]
        conv = low(total_conv)
        conv_ref[...] = conv
        recur = jax.nn.sigmoid(matmul(conv, aw_ref[0]) + ab_ref[...])
        gate = jax.nn.sigmoid(matmul(conv, iw_ref[0]) + ib_ref[...])
        recur_ref[...] = recur
        input_ref[...] = gate
        log_decay = -8.0 * recur * soft_ref[...]
        scaling = jnp.where(masks_ref[:, taps + 1:taps + 2] > 0.5, 1.0, root_of(log_decay))
        columns = pl.ds(pl.multiple_of(head * block, block), block)
        decay[:, columns] = jnp.exp(log_decay) * masks_ref[:, taps:taps + 1]
        driven[:, columns] = scaling * gate * conv.astype(jnp.float32)

        @pl.when(head == heads - 1)
        def _():
            product, state = run_scan(decay, driven, product_ref, state_ref, False)
            end_ref[0:1, :] = product
            end_ref[1:2, :] = state

    by_head = lambda rows: pl.BlockSpec((rows, block), lambda h: (0, h))
    square = pl.BlockSpec((1, block, block), lambda h: (h, 0, 0))
    fixed = lambda shape: pl.BlockSpec(shape, lambda h: (0, 0))
    real = jnp.float32
    return pl.pallas_call(kernel, grid=(heads,), out_shape=[jax.ShapeDtypeStruct((length, width), jnp.bfloat16), jax.ShapeDtypeStruct((length, width), real), jax.ShapeDtypeStruct((length, width), real), jax.ShapeDtypeStruct((length, width), real), jax.ShapeDtypeStruct((length, width), real), jax.ShapeDtypeStruct((2, width), real)], in_specs=[by_head(length), by_head(pad), fixed(masks.shape), by_head(taps), square, by_head(1), square, by_head(1), by_head(1)], out_specs=[by_head(length)] * 3 + [fixed((length, width))] * 2 + [fixed((2, width))], scratch_shapes=[pltpu.VMEM((length + pad, block), real), pltpu.VMEM((length, width), real), pltpu.VMEM((length, width), real)])(branch, edge, masks, conv_weight, a_weight, a_bias, i_weight, i_bias, softened)

def lru_turn(parts, y_branch, states, recur, masks, softened, total_product, block):
    length, width = states.shape
    heads = width // block
    keep = masks.shape[1] - 2

    def kernel(*refs):
        part_refs = refs[:len(parts)]
        y_ref, state_ref, recur_ref, masks_ref, soft_ref, product_ref = refs[len(parts):-6]
        y_grad_ref, delta_ref, later_ref, end_ref, decay, term = refs[-6:]
        head = pl.program_id(0)
        columns = pl.ds(pl.multiple_of(head * block, block), block)
        mixed_grad = part_refs[0][...].astype(jnp.float32)
        for part in part_refs[1:]:
            mixed_grad = mixed_grad + part[...].astype(jnp.float32)
        mixed_grad = low(mixed_grad).astype(jnp.float32)
        value = y_ref[...].astype(jnp.float32)
        square = value * value
        bend = jnp.tanh(0.7978845608028654 * (value + 0.044715 * square * value))
        slope = 0.5 * (1.0 + bend) + 0.5 * value * (1.0 - bend * bend) * 0.7978845608028654 * (1.0 + 3.0 * 0.044715 * square)
        y_grad_ref[...] = low(mixed_grad * state_ref[...] * slope)
        term[:, columns] = mixed_grad * (0.5 * value * (1.0 + bend))
        decay[pl.ds(0, length), columns] = jnp.exp(-8.0 * recur_ref[...] * soft_ref[...]) * masks_ref[:, keep:keep + 1]
        decay[pl.ds(length, 1), columns] = jnp.ones((1, block), jnp.float32)

        @pl.when(head == heads - 1)
        def _():
            _, delta = run_scan(decay, term, later_ref, delta_ref, True)
            end_ref[0:1, :] = product_ref[...]
            end_ref[1:2, :] = decay[0:1, :] * delta

    by_head = lambda rows: pl.BlockSpec((rows, block), lambda h: (0, h))
    fixed = lambda shape: pl.BlockSpec(shape, lambda h: (0, 0))
    real = jnp.float32
    return pl.pallas_call(kernel, grid=(heads,), out_shape=[jax.ShapeDtypeStruct((length, width), jnp.bfloat16), jax.ShapeDtypeStruct((length, width), real), jax.ShapeDtypeStruct((length, width), real), jax.ShapeDtypeStruct((2, width), real)], in_specs=[by_head(length)] * (len(parts) + 3) + [fixed(masks.shape), by_head(1), fixed((1, width))], out_specs=[by_head(length)] + [fixed((length, width))] * 2 + [fixed((2, width))], scratch_shapes=[pltpu.VMEM((length + 8, width), real), pltpu.VMEM((length, width), real)])(*parts, y_branch, states, recur, masks, softened, total_product)

def lru_back(deltas_local, later, grad_in, states, state_in, conv, recur, gate, branch, edge, masks, conv_weight, a_weight, i_weight, softened):
    length, width = states.shape
    heads, block, _ = a_weight.shape
    taps = conv_weight.shape[0]
    pad = edge.shape[0]

    def kernel(delta_ref, later_ref, grad_in_ref, state_ref, state_in_ref, conv_ref, recur_ref, gate_ref, branch_ref, edge_ref, masks_ref, taps_ref, aw_ref, iw_ref, soft_ref, main_ref, halo_ref, sums_ref, gates_ref, extended, gathered):
        delta = delta_ref[...] + later_ref[...] * grad_in_ref[...]
        extended[pl.ds(pad - 1, 1), :] = state_in_ref[...]
        extended[pl.ds(pad, length), :] = state_ref[...]
        previous = extended[pl.ds(pad - 1, length), :]
        recur = recur_ref[...]
        gate = gate_ref[...]
        soft = soft_ref[...]
        conv_low = conv_ref[...]
        conv = conv_low.astype(jnp.float32)
        keeping = masks_ref[:, taps:taps + 1]
        reset = masks_ref[:, taps + 1:taps + 2] > 0.5
        log_decay = -8.0 * recur * soft
        raw = jnp.exp(log_decay)
        root = root_of(log_decay)
        scaling = jnp.where(reset, 1.0, root)
        conv_grad = delta * scaling * gate
        log_grad = delta * previous * keeping * raw - jnp.where(reset, 0.0, delta * gate * conv * (raw * raw) / root)
        a_grad = low(log_grad * (-8.0 * soft) * recur * (1.0 - recur))
        i_grad = low(delta * scaling * conv * gate * (1.0 - gate))
        rows = [None] * 8
        rows[taps] = jnp.sum(a_grad.astype(jnp.float32), axis=0, keepdims=True)
        rows[taps + 1] = jnp.sum(i_grad.astype(jnp.float32), axis=0, keepdims=True)
        rows[taps + 2] = jnp.sum(log_grad * (-8.0 * recur), axis=0, keepdims=True)
        gates_ref[0] = low(outer_sum(conv_low, a_grad))
        gates_ref[1] = low(outer_sum(conv_low, i_grad))
        conv_grad = conv_grad + (times_transposed(a_grad, aw_ref[0]) + times_transposed(i_grad, iw_ref[0]))
        extended[pl.ds(0, pad), :] = edge_ref[...].astype(jnp.float32)
        extended[pl.ds(pad, length), :] = branch_ref[...].astype(jnp.float32)
        gathered[...] = jnp.zeros(gathered.shape, jnp.float32)
        for k in range(taps):
            masked = conv_grad * masks_ref[:, k:k + 1]
            rows[k] = jnp.sum(masked * extended[pl.ds(pad - k, length), :], axis=0, keepdims=True)
            place = pl.ds(pad - k, length)
            gathered[place, :] = gathered[place, :] + masked * taps_ref[k:k + 1, :]
        for k in range(8):
            sums_ref[k:k + 1, :] = jnp.zeros((1, block), jnp.float32) if rows[k] is None else rows[k]
        main_ref[...] = gathered[pl.ds(pad, length), :]
        halo_ref[...] = gathered[pl.ds(0, pad), :]

    by_head = lambda rows: pl.BlockSpec((rows, block), lambda h: (0, h))
    square = pl.BlockSpec((1, block, block), lambda h: (h, 0, 0))
    fixed = lambda shape: pl.BlockSpec(shape, lambda h: (0, 0))
    real = jnp.float32
    return pl.pallas_call(kernel, grid=(heads,), out_shape=[jax.ShapeDtypeStruct((length, width), real), jax.ShapeDtypeStruct((pad, width), real), jax.ShapeDtypeStruct((8, width), real), jax.ShapeDtypeStruct((2, heads * block, block), jnp.bfloat16)], in_specs=[by_head(length), by_head(length), by_head(1), by_head(length), by_head(1), by_head(length), by_head(length), by_head(length), by_head(length), by_head(pad), fixed(masks.shape), by_head(taps), square, square, by_head(1)], out_specs=[by_head(length), by_head(pad), by_head(8), pl.BlockSpec((2, block, block), lambda h: (0, h, 0))], scratch_shapes=[pltpu.VMEM((length + pad, block), real), pltpu.VMEM((length + pad, block), real)])(deltas_local, later, grad_in, states, state_in, conv, recur, gate, branch, edge, masks, conv_weight, a_weight, i_weight, softened)

def piece_products(terms, size, count):
    arrays, plan = ([], [])
    for left, left_start, right, right_start in terms:
        places = []
        for array in (left, right):
            known = [i for i, other in enumerate(arrays) if other is array]
            if not known:
                arrays.append(array)
            places.append(known[0] if known else len(arrays) - 1)
        rows = min(left.shape[1] - left_start, right.shape[0] - right_start)
        plan.append((places[0], left_start, places[1], right_start, rows))
    height = terms[0][0].shape[0]

    def kernel(*refs):
        out_refs = refs[len(arrays):]
        for place in range(count):
            result = None
            for left, left_start, right, right_start, rows in plan:
                term = matmul(refs[left][:, left_start:left_start + rows], refs[right][right_start:right_start + rows, place * size:(place + 1) * size])
                result = term if result is None else result + term
            out_refs[place][...] = low(result)

    return pl.pallas_call(kernel, out_shape=[jax.ShapeDtypeStruct((height, size), jnp.bfloat16)] * count, in_specs=[whole()] * len(arrays))(*arrays)

def weight_copies(refs, weights, arrived):
    copies = [pltpu.make_async_copy(ref, weights.at[i], arrived.at[i]) for i, ref in enumerate(refs)]
    for copy in copies:
        copy.start()
    return copies

def forward_products(rows, gate_pieces, up_pieces, early):
    tokens, _ = rows.shape
    units, piece = gate_pieces[0].shape
    places = list(early) + list(early)

    def kernel(*refs):
        rows_ref = refs[0]
        piece_refs = refs[1:1 + len(places)]
        gates, ups, weights, arrived = refs[-4:]
        copies = weight_copies(piece_refs, weights, arrived)

        def add(target, first, last):
            for i in range(first, last):
                copies[i].wait()
                start = places[i] * piece
                term = times_transposed(weights[i], rows_ref[:, start:start + piece])
                target[...] = term if i == first else target[...] + term

        add(gates, 0, len(early))
        add(ups, len(early), len(places))

    return pl.pallas_call(kernel, out_shape=[jax.ShapeDtypeStruct((units, tokens), jnp.float32)] * 2, in_specs=[whole()] + [pl.BlockSpec(memory_space=pl.ANY)] * len(places), out_specs=[whole()] * 2, scratch_shapes=[pltpu.VMEM((len(places), units, piece), jnp.bfloat16), pltpu.SemaphoreType.DMA((len(places),))])(rows, *[gate_pieces[p] for p in early], *[up_pieces[p] for p in early])

def feed_forward(rows, gates, ups, hidden_parts, gate_pieces, up_pieces, late):
    tokens, width = rows.shape
    units, piece = gate_pieces[0].shape
    count = len(gate_pieces)
    half = tokens // 2
    tile = 16
    chunk = 128
    order = list(late) + [count + p for p in late]
    order += [i for i in range(2 * count) if i not in order]
    place_of = {which: place for place, which in enumerate(order)}
    pieces = list(gate_pieces) + list(up_pieces)

    def kernel(*refs):
        rows_ref, gates, ups = refs[:3]
        part_refs = refs[3:3 + len(hidden_parts)]
        piece_refs = refs[3 + len(hidden_parts):3 + len(hidden_parts) + 2 * count]
        hidden_ref, gate_ref, up_ref, near_ref, other_ref = refs[-11:-6]
        weights, all_gates, all_ups, turned_gate, turned_up, arrived = refs[-6:]
        copies = weight_copies(piece_refs, weights, arrived)
        for target, start, first in ((all_gates, gates, 0), (all_ups, ups, len(late))):
            result = start[...]
            for place, p in enumerate(late):
                copies[first + place].wait()
                result = result + times_transposed(weights[first + place], rows_ref[:, p * piece:(p + 1) * piece])
            target[...] = result

        def step(index, carried):
            place = pl.ds(pl.multiple_of(index * tile, tile), tile)

            def inner(part, carried):
                columns = pl.ds(pl.multiple_of(part * chunk, chunk), chunk)
                back = part_refs[0][place, columns].astype(jnp.float32)
                for ref in part_refs[1:]:
                    back = back + ref[place, columns].astype(jnp.float32)
                back = low(back).astype(jnp.float32)
                value = all_gates[place, columns]
                up = all_ups[place, columns]
                square = value * value
                bend = jnp.tanh(0.7978845608028654 * (value + 0.044715 * square * value))
                act = 0.5 * value * (1.0 + bend)
                slope = 0.5 * (1.0 + bend) + 0.5 * value * (1.0 - bend * bend) * 0.7978845608028654 * (1.0 + 3.0 * 0.044715 * square)
                hidden_ref[place, columns] = low(act * up)
                gate_ref[place, columns] = low(back * up * slope)
                up_ref[place, columns] = low(back * act)
                return carried

            return lax.fori_loop(0, tokens // chunk, inner, carried, unroll=4)

        lax.fori_loop(0, units // tile, step, 0)
        turned_gate[...] = gate_ref[...].T
        turned_up[...] = up_ref[...].T
        for copy in copies[2 * len(late):]:
            copy.wait()
        for i in range(count):
            columns = slice(i * piece, (i + 1) * piece)
            result = low(matmul(turned_gate[...], weights[place_of[i]]) + matmul(turned_up[...], weights[place_of[count + i]]))
            near_ref[:, columns] = result[:half]
            other_ref[:, columns] = result[half:]

    low_shape = lambda *shape: jax.ShapeDtypeStruct(shape, jnp.bfloat16)
    anywhere = pl.BlockSpec(memory_space=pl.ANY)
    return pl.pallas_call(kernel, out_shape=[low_shape(units, tokens)] * 3 + [low_shape(half, width)] * 2, in_specs=[whole()] * (3 + len(hidden_parts)) + [anywhere] * (2 * count), scratch_shapes=[pltpu.VMEM((2 * count, units, piece), jnp.bfloat16), pltpu.VMEM((units, tokens), jnp.float32), pltpu.VMEM((units, tokens), jnp.float32), pltpu.VMEM((tokens, units), jnp.bfloat16), pltpu.VMEM((tokens, units), jnp.bfloat16), pltpu.SemaphoreType.DMA((2 * count,))])(rows, gates, ups, *hidden_parts, *[pieces[i] for i in order])

def stacked_kernel(groups, weights, outputs, finish, extra=(), scratch=()):
    shapes = [(sum((part.shape[0] for part in parts)), parts[0].shape[1]) for parts in groups]
    flat = [part for parts in groups for part in parts]

    def kernel(*refs):
        extra_refs = refs[:len(extra)]
        part_refs = list(refs[len(extra):len(extra) + len(flat)])
        rest = refs[len(extra) + len(flat):]
        weight_refs = rest[:len(weights)]
        out_refs = rest[len(weights):len(weights) + len(outputs)]
        holders = rest[len(weights) + len(outputs):]
        for parts, holder in zip(groups, holders):
            row = 0
            for part in parts:
                holder[row:row + part.shape[0], :] = part_refs.pop(0)[...]
                row += part.shape[0]
        finish(extra_refs, holders[:len(groups)], weight_refs, out_refs, holders[len(groups):])

    return pl.pallas_call(kernel, out_shape=outputs, in_specs=[pl.BlockSpec(memory_space=pltpu.SMEM)] * len(extra) + [whole()] * (len(flat) + len(weights)), scratch_shapes=[pltpu.VMEM(shape, jnp.bfloat16) for shape in shapes] + list(scratch))(*extra, *flat, *weights)

def gather_sums(sums, gains):
    count = lax.axis_size(at_batch)
    width = sums.shape[1]
    pieces = gains[0].shape[1] // count
    mine = lax.axis_index(at_batch).astype(jnp.int32).reshape(1)
    per_row = width // pieces
    above = sums.shape[0]
    rows = above + len(gains) * (count // per_row)

    def kernel(mine_ref, sums_ref, *refs):
        out_ref = refs[-1]
        out_ref[:above, :] = sums_ref[...]
        for i in range(len(gains)):
            for j in range(count):
                row = above + i * (count // per_row) + j // per_row
                left = j % per_row * pieces
                for k in range(count):

                    @pl.when(jnp.bitwise_xor(mine_ref[0], j) == k)
                    def _():
                        out_ref[row:row + 1, left:left + pieces] = refs[i][:, k * pieces:(k + 1) * pieces]

    return pl.pallas_call(kernel, out_shape=jax.ShapeDtypeStruct((rows, width), jnp.float32), in_specs=[pl.BlockSpec(memory_space=pltpu.SMEM)] + [whole()] * (1 + len(gains)))(mine, sums, *gains)

def side_by_side(parts):
    columns = parts[0].shape[1]

    def kernel(*refs):
        for i in range(len(parts)):
            refs[-1][:, i * columns:(i + 1) * columns] = refs[i][...]

    return pl.pallas_call(kernel, out_shape=jax.ShapeDtypeStruct((parts[0].shape[0], columns * len(parts)), parts[0].dtype), in_specs=[whole()] * len(parts))(*parts)

def home_product(groups, weights, transposed, length):
    half = length // 2
    count = len(groups[0])
    columns = weights[0].shape[0] if transposed else weights[0].shape[1]
    core = lax.axis_index(at_tensor).astype(jnp.int32).reshape(1)

    def finish(extra_refs, holders, weight_refs, out_refs, scratch):
        multiply = times_transposed if transposed else matmul
        result = None
        for holder, weight in zip(holders, weight_refs):
            term = multiply(holder[...], weight[...])
            result = term if result is None else result + term
        scratch[0][...] = result
        for k in range(count):
            for out_ref, turn in zip(out_refs, (0, 1)):
                start = k * length + half * jnp.bitwise_xor(extra_refs[0][0], turn)
                rows = scratch[0][pl.ds(pl.multiple_of(start, half), half), :]
                out_ref[k * half:(k + 1) * half, :] = rows.astype(out_ref.dtype)

    return stacked_kernel(groups, weights, [jax.ShapeDtypeStruct((count * half, columns), jnp.float32), jax.ShapeDtypeStruct((count * half, columns), jnp.bfloat16)], finish, (core,), (pltpu.VMEM((count * length, columns), jnp.float32),))

def piece_grads(rights, parts, length):
    count = len(parts)
    size = parts[0].shape[0]
    blocks = parts[0].shape[1] // (2 * length)
    share = count // 2
    height = share * length
    columns = rights[0][0].shape[1]
    core = lax.axis_index(at_tensor).astype(jnp.int32).reshape(1)

    def kernel(core_ref, *refs):
        right_refs = refs[:2 * blocks]
        part_refs = refs[2 * blocks:2 * blocks + count]
        out_ref, holder = refs[-2:]
        for side in range(2):
            for k in range(blocks):
                for step in range(share):
                    row = k * height + step * length
                    source = right_refs[side * blocks + k]
                    place = jnp.bitwise_xor(core_ref[0], side) * share + step
                    start = place * (blocks * length) + k * length
                    holder[pl.ds(pl.multiple_of(start, length), length), :] = source[step * length:(step + 1) * length, :]
        for which in range(2):
            result = None
            for j in range(count):
                for k in range(blocks):
                    source = (2 * k + which) * length
                    row = (j * blocks + k) * length
                    term = matmul(part_refs[j][:, source:source + length], holder[row:row + length, :])
                    result = term if result is None else result + term
            out_ref[which * size:(which + 1) * size, :] = low(result)

    return pl.pallas_call(kernel, out_shape=jax.ShapeDtypeStruct((2 * size, columns), jnp.bfloat16), in_specs=[pl.BlockSpec(memory_space=pltpu.SMEM)] + [whole()] * (2 * blocks + count), scratch_shapes=[pltpu.VMEM((count * blocks * length, columns), jnp.bfloat16)])(core, *rights[0], *rights[1], *parts)

def seq_pieces(arrays):
    count = lax.axis_size(at_seq)
    length, width = arrays[0].shape
    size = width // count
    mine = lax.axis_index(at_seq).astype(jnp.int32).reshape(1)

    def kernel(mine_ref, *refs):
        in_refs = refs[:len(arrays)]
        out_refs = refs[len(arrays):len(arrays) + count]
        turned_ref = refs[-1]
        for i, ref in enumerate(in_refs):
            turned_ref[:, i * length:(i + 1) * length] = ref[...].T
        for k in range(count):
            start = jnp.bitwise_xor(mine_ref[0], k) * size
            out_refs[k][...] = turned_ref[pl.ds(pl.multiple_of(start, size), size), :]

    shape = (size, length * len(arrays))
    return pl.pallas_call(kernel, out_shape=[jax.ShapeDtypeStruct(shape, arrays[0].dtype)] * count, in_specs=[pl.BlockSpec(memory_space=pltpu.SMEM)] + [whole()] * len(arrays), scratch_shapes=[pltpu.VMEM((width, length * len(arrays)), arrays[0].dtype)])(mine, *arrays)

def joined(relative):
    count = len(relative)
    size, rows = relative[0].shape
    size //= 2
    mine = lax.axis_index(at_seq).astype(jnp.int32).reshape(1)

    def kernel(mine_ref, *refs):
        for which, out_ref in enumerate(refs[-2:]):

            @pl.when(pl.program_id(0) == which)
            def _():
                for k in range(count):
                    value = refs[k][...].T.astype(jnp.float32)
                    for j in range(count):

                        @pl.when(jnp.bitwise_xor(mine_ref[0], j) == k)
                        def _():
                            out_ref[:, j * size:(j + 1) * size] = value

    return pl.pallas_call(kernel, grid=(2,), out_shape=[jax.ShapeDtypeStruct((rows, size * count), jnp.float32)] * 2, in_specs=[pl.BlockSpec(memory_space=pltpu.SMEM)] + [pl.BlockSpec((size, rows), lambda i: (i, 0))] * count, out_specs=[pl.BlockSpec((rows, size * count), lambda i: (0, 0))] * 2)(mine, *relative)

def entering(both, direction, reach):
    arrived = [shifted(both, at_seq, direction * (d + 1)) for d in range(reach)]
    carried = arrived[-1][1:2]
    for pair in arrived[-2::-1]:
        carried = pair[1:2] + pair[0:1] * carried
    return carried

def all_rows(own):
    near = jnp.concatenate(along_line(own))
    other = swap(near, at_tensor, 1)
    return (near, jnp.concatenate([near, other]))

def own_rows(mine, given, finish):
    count = lax.axis_size(at_seq)
    other = swap(given, at_tensor, 1)
    near = low(mine.astype(jnp.float32) + other.astype(jnp.float32))
    rows = near.shape[0] // count
    return onto_line([near[k * rows:(k + 1) * rows] for k in range(count)], finish=finish)

def column_class(values, index):
    width = values.shape[1] // lax.axis_size(at_batch)
    steps = [0] + list(far_steps())
    return jnp.concatenate([values[:, (k + index) * width:(k + index + 1) * width] for k in steps], axis=1)

def paired_rows(own):
    steps = near_steps()
    parts = trade([column_class(own, i) for i in range(len(steps) + 1)], at_batch, steps)
    near = jnp.stack(along_line(jnp.stack(parts)))
    other = swap(near, at_tensor, 1)
    both = jnp.stack([near, other])
    return both.transpose(2, 0, 1, 3, 4).reshape(-1, near.shape[3])

def paired_sums(partials, half):
    count = lax.axis_size(at_seq)
    here = count * half
    other = swap(jnp.stack([low(part[here:]) for part in partials]), at_tensor, 1)
    mine = jnp.stack([part[:here] for part in partials])
    near = low(mine + other.astype(jnp.float32))
    return near.reshape(len(partials), count, half, -1)

def own_from_paired(near, gate):
    steps = near_steps()
    groups = len(steps) + 1
    count = lax.axis_size(at_seq)
    mine = low(onto_line([near[:, k] for k in range(count)], gate))
    parts = trade([mine[i] for i in range(groups)], at_batch, steps)
    width = parts[0].shape[1] // (len(far_steps()) + 1)
    return jnp.concatenate([parts[k % groups][:, k // groups * width:(k // groups + 1) * width] for k in range(lax.axis_size(at_batch))], axis=1)

def plane_rows(own):
    near = jnp.stack(trade_columns(own))
    other = swap(near, at_tensor, 1)
    first = lax.axis_index(at_tensor) == 0
    upper = jnp.where(first, near, other)
    lower = jnp.where(first, other, near)
    return jnp.concatenate([upper, lower], axis=1).reshape(-1, near.shape[2])

def trade_columns(rows):
    count = lax.axis_size(at_batch)
    width = rows.shape[1] // count
    return trade([rows[:, k * width:(k + 1) * width] for k in range(count)], at_batch)

def home_rows(keep, give):
    count = lax.axis_size(at_batch)
    other = swap(give, at_tensor, 1)
    near = low(keep + other.astype(jnp.float32))
    half = near.shape[0] // count
    parts = trade([near[k * half:(k + 1) * half] for k in range(count)], at_batch)
    return jnp.concatenate(parts, axis=1)

def both_halves(own):
    other = swap(own, at_tensor, 1)
    first = lax.axis_index(at_tensor) == 0
    return jnp.concatenate([jnp.where(first, own, other), jnp.where(first, other, own)])

def seq_sum(partial, finish):
    count = lax.axis_size(at_seq)
    mine = lax.axis_index(at_seq)
    rows = partial.shape[0] // count
    shared = low(partial)
    mine_sum = onto_line([pick(shared, jnp.bitwise_xor(mine, k), rows, 0) for k in range(count)], finish=finish)
    spread_out = along_line(low(mine_sum))
    return jnp.concatenate(ordered(spread_out, at_seq)).astype(jnp.float32)

def spread_pieces(pieces, gate):
    arrived = trade(pieces, at_seq)
    arrived = list(lax.optimization_barrier((*arrived, gate))[:-1])
    return spread(side_by_side(arrived), at_batch)

def grid_sum(values):
    stages = [(at_batch, [0] + list(far_steps()), near_count()), (at_batch, [0] + list(near_steps()), 1)]
    back = []
    for axis, steps, unit in stages:
        count = len(steps)
        mine = lax.axis_index(axis) // unit % count
        rows = values.shape[0] // count
        parts = [pick(values, jnp.bitwise_xor(mine, i), rows, 0) for i in range(count)]
        parts = trade(parts, axis, steps[1:])
        values = low(total(parts))
        back.append((axis, steps, mine))
    count = lax.axis_size(at_seq)
    mine = lax.axis_index(at_seq)
    rows = values.shape[0] // count
    parts = [pick(values, jnp.bitwise_xor(mine, k), rows, 0) for k in range(count)]
    parts = trade(parts, at_seq)
    values = low(total(parts))
    back.append((at_seq, list(range(count)), mine))
    for axis, steps, mine in back[::-1]:
        parts = spread(values, axis, steps[1:])
        stacked = jnp.stack(parts)
        values = jnp.concatenate([lax.dynamic_index_in_dim(stacked, jnp.bitwise_xor(mine, j), 0, keepdims=False) for j in range(len(steps))])
    return values

def per_device(tokens, segment_ids, norm1_gain, x_weight, y_weight, conv_weight, a_gate_weight, a_gate_bias, in_gate_weight, in_gate_bias, decay_param, out_weight, norm2_gain, gate_weight, up_weight, down_weight, out_grad):
    length = tokens.shape[1]
    width = tokens.shape[2]
    half = length // 2
    taps = conv_weight.shape[0]
    heads = a_gate_weight.shape[0]
    block_size = a_gate_weight.shape[1]
    seq_index = lax.axis_index(at_seq)
    core = lax.axis_index(at_tensor)
    planes = lax.axis_size(at_batch)
    reach = min(lax.axis_size(at_seq) - 1, -(-longest_document // length))
    tokens_turned = turned(tokens.reshape(length, width))
    cotangent_half = turned(pick(out_grad.reshape(length, width), core, half, 0))
    gain_one = turned(norm1_gain)
    gain_two = turned(norm2_gain)
    inputs = tokens_turned.astype(jnp.float32)
    position = seq_index * length
    marks = jnp.concatenate([jnp.full((taps - 1,), -1, jnp.int32), segment_ids.reshape(-1)])
    nearby = lax.dynamic_slice_in_dim(marks, position, length + taps - 1)
    current = nearby[taps - 1:]
    reset = current != nearby[taps - 2:taps - 2 + length]
    keeping = (1.0 - reset.astype(jnp.float32))[:, None]
    same_docs = [(nearby[taps - 1 - offset:taps - 1 - offset + length] == current).astype(jnp.float32)[:, None] for offset in range(taps)]
    masks = jnp.concatenate(same_docs + [keeping, reset.astype(jnp.float32)[:, None]], axis=1)
    softened = jax.nn.softplus(decay_param)[None]
    a_bias_row = a_gate_bias[None]
    in_bias_row = in_gate_bias[None]
    normed = low(rms_scale(inputs, gain_one))
    normed_parts = trade_columns(normed)
    normed_plane = jnp.concatenate(normed_parts)
    x_part = low(matmul(normed_plane, x_weight))
    y_part = low(matmul(after(normed_plane, x_part), y_weight))
    x_parts = trade([x_part[k * length:(k + 1) * length] for k in range(planes)], at_batch)
    y_parts = trade([y_part[k * length:(k + 1) * length] for k in range(planes)], at_batch)
    x_branch = low(total(x_parts))
    y_branch = low(total(y_parts))
    cotangent_pair = paired_rows(after(cotangent_half, normed))
    every_own = pick(normed_plane, core, normed_plane.shape[0] // 2, 0)
    every_near = spread(every_own, at_seq)
    every_other = [swap(part, at_tensor, 1) for part in every_near]
    every = (every_near, every_other)
    gate_first = spread(after(gate_weight.T, normed), at_batch, near_steps())
    up_first = spread(after(up_weight.T, normed), at_batch, far_steps())
    gate_second = spread(gate_first[0], at_batch, far_steps())
    up_second = spread(up_first[0], at_batch, near_steps())
    down_parts = spread(after(down_weight, x_part), at_batch, far_steps())
    weight_down = jnp.concatenate(down_parts, axis=1)
    hidden_part = low(times_transposed(weight_down, cotangent_pair))
    edge = shifted(x_branch[length - 8:], at_seq, 1)
    conv_low, recur_gate, input_gate, products, local_states, ends = lru_ahead(x_branch, edge, masks, conv_weight, a_gate_weight, a_bias_row, in_gate_weight, in_bias_row, softened)
    state_in = entering(ends, 1, reach)
    states = local_states + products * state_in
    mixed = low(states * gelu_tanh(y_branch.astype(jnp.float32)))
    mixed_parts = spread(mixed, at_batch)
    far = len(far_steps()) + 1
    near = near_count()
    rows = gate_weight.shape[0]
    gate_rest = [spread(piece, at_batch, far_steps()) for piece in gate_first[1:]]
    up_rest = [spread(piece, at_batch, near_steps()) for piece in up_first[1:]]
    gate_rest = [gate_second] + gate_rest
    up_rest = [up_second] + up_rest
    gate_pieces = [column[i] for i in range(far) for column in gate_rest]
    up_pieces = [piece for row in up_rest for piece in row]
    tokens_here = 2 * lax.axis_size(at_seq) * half
    hidden_parts = trade([hidden_part[:, i * tokens_here:(i + 1) * tokens_here] for i in range(near)], at_batch, near_steps())
    inputs_half = pick(inputs, core, half, 0)
    home_parts = home_product([mixed_parts], [out_weight], False, length)
    middle = inputs_half + home_rows(*home_parts).astype(jnp.float32)
    normed_two_near, normed_two_all = all_rows(low(rms_scale(middle, gain_two)))
    group = near * (width // planes)
    pair_near = trade([normed_two_near[:, f * group:(f + 1) * group] for f in range(far)], at_batch, far_steps())[1:]
    pair_other = [swap(part, at_tensor, 1) for part in pair_near]
    late = [f * near + i for f in range(1, far) for i in range(1, near)]
    early = [p for p in range(planes) if p not in late]
    gates_pre, ups_pre = forward_products(normed_two_all, gate_pieces, up_pieces, early)
    hidden, gate_grad, up_grad, near_part, other_part = feed_forward(normed_two_all, gates_pre, ups_pre, hidden_parts, gate_pieces, up_pieces, late)
    hidden_both = spread(hidden, at_batch, near_steps())
    gate_far = spread(gate_grad, at_batch, far_steps())[1:]
    up_far = spread(up_grad, at_batch, far_steps())[1:]

    def pair_terms(own, others):
        terms = [(own, 0, normed_two_all, 0)]
        for other, here, there in zip(others, pair_near, pair_other):
            terms += [(other, 0, here, 0), (other, here.shape[0], there, 0)]
        return terms

    gate_far = [after(part, pair_other[0]) for part in gate_far]
    gate_full = piece_products(pair_terms(gate_grad, gate_far), rows, near)
    gate_parts = trade(gate_full, at_batch, near_steps())
    sum_gate = total(gate_parts).T
    up_full = piece_products(pair_terms(up_grad, up_far), rows, near)
    up_parts = trade(up_full, at_batch, near_steps())
    sum_up = total(up_parts).T
    hidden_both = hidden_both[:1] + [after(part, pair_other[0]) for part in hidden_both[1:]]
    out_parts = [outer_sum(part, weight_down) for part in hidden_both]
    out_sums = paired_sums(out_parts, half)
    normed_two_grad = own_rows(near_part, other_part, None)
    tokens_here = hidden.shape[1]
    down_full = piece_products([(part, 0, cotangent_pair, i * tokens_here) for i, part in enumerate(hidden_both)], down_weight.shape[1], far)
    down_parts = trade(down_full, at_batch, far_steps())
    sum_down = total(down_parts)
    back_two, grad_norm2 = norm_back(middle, gain_two, normed_two_grad)
    middle_grad = cotangent_half.astype(jnp.float32) + back_two
    branch_plane = plane_rows(low(middle_grad))
    do_part = low(times_transposed(branch_plane, out_weight))
    do_parts = trade([do_part[k * length:(k + 1) * length] for k in range(planes)], at_batch)
    grad_out = outer_sum(jnp.concatenate(mixed_parts), after(branch_plane, do_part))
    y_grad, local_deltas, later_products, back_ends = lru_turn(do_parts, y_branch, states, recur_gate, masks, softened, ends[0:1], block_size)
    y_grad_parts = spread(y_grad, at_batch)
    grad_in = entering(back_ends, -1, reach)
    main_grad, halo, sums, gates = lru_back(local_deltas, later_products, grad_in, states, state_in, conv_low, recur_gate, input_gate, x_branch, edge, masks, conv_weight, a_gate_weight, in_gate_weight, softened)
    arriving = shifted(halo, at_seq, -1)
    x_grad = low(main_grad + jnp.pad(arriving, ((length - 8, 0), (0, 0))))
    x_grad_parts = spread(x_grad, at_batch)
    home_parts = home_product([y_grad_parts, x_grad_parts], [y_weight, x_weight], True, length)
    normed_grad = home_rows(*home_parts).astype(jnp.float32)
    back_one, grad_norm1 = norm_back(inputs_half, gain_one, normed_grad)
    tokens_grad = turned(both_halves(middle_grad + back_one)).reshape(tokens.shape)
    sum_out = seq_sum(grad_out, None)
    pieces = seq_pieces([y_grad, x_grad])
    pieces = spread_pieces(pieces, x_grad)
    sum_y, sum_x = joined(along_line(piece_grads(every, pieces, length)))
    result = middle + own_from_paired(out_sums, branch_plane).astype(jnp.float32)
    block_out = turned(both_halves(low(result))).reshape(tokens.shape)
    gates = grid_sum(gates.reshape(-1, block_size)).astype(jnp.float32)
    gates = gates.reshape(2, heads, block_size, block_size)
    both_gains = jnp.concatenate([grad_norm1[None], grad_norm2[None]])
    both_gains = both_gains + swap(both_gains, at_tensor, 1)
    vectors = gather_sums(sums, [both_gains[0:1], both_gains[1:2]])
    vectors = butterfly(vectors, (at_batch,))
    vectors = sum(spread(vectors, at_seq))
    gains = vectors[sums.shape[0]:].reshape(2, width)
    return (block_out, tokens_grad, gains[0], sum_x, sum_y, vectors[:taps], gates[0], vectors[taps], gates[1], vectors[taps + 1], vectors[taps + 2] * jax.nn.sigmoid(decay_param), sum_out, gains[1], sum_gate, sum_up, sum_down)


def solution(mesh):
    return jax.shard_map(per_device, mesh=mesh, in_specs=(P(at_batch, at_seq, None), P(at_batch, None), P(), P(at_batch, at_tensor), P(at_batch, at_tensor), P(None, at_tensor), P(at_tensor, None, None), P(at_tensor), P(at_tensor, None, None), P(at_tensor), P(at_tensor), P(at_tensor, at_batch), P(), P(at_batch, (at_seq, at_tensor)), P(at_batch, (at_seq, at_tensor)), P((at_seq, at_tensor), at_batch), P(at_batch, at_seq, None)), out_specs=(P(at_batch, at_seq, None), P(at_batch, at_seq, None), P(), P(at_batch, at_tensor), P(at_batch, at_tensor), P(None, at_tensor), P(at_tensor, None, None), P(at_tensor), P(at_tensor, None, None), P(at_tensor), P(at_tensor), P(at_tensor, at_batch), P(), P(at_batch, (at_seq, at_tensor)), P(at_batch, (at_seq, at_tensor)), P((at_seq, at_tensor), at_batch)), check_vma=False)
```
